32 devices in a mesh: param: 4 (over y, core), ex: 8 (over z, x).
Axes of the slice: x: 2, y: 2, z: 4, core: 2. Of those that a mesh axis runs over, the one named last changes fastest.
Arguments:
- activations: bfloat16 [512, 128, 8192], P('ex', None, 'param'), may hold values from -8 to 8
- cotangents: bfloat16 [512, 128, 64], P('ex'), may hold values from -8 to 8
- token_ids: int32 [512, 128], P('ex'), may hold values from 0 to 128255, as said below
- signs: int32 [64, 8192], P(None, 'param'), may hold values from -1 to 1, as said below
- select: int32 [32768], replicated, may hold values from 0 to 524287, as said below
Outputs:
- features: float32 [512, 32768], P('ex', 'param')
- gram: float32 [512, 512], P('ex')
The draws below stay inside these ranges and needn't reach their ends.
Inputs may be any that keep to these rules, and one draw needn't show every extreme that they name: `token_ids`: in each example the nonzero ids come first and zeros fill the rest; at least 32 positions of every example are nonzero. `signs`: every entry is 1 or -1. `select`: the 32768 entries are distinct.
All inputs are finite; a program needn't handle non-finite values.
Results may differ from the reference program's by a relative error of at most 0.0003.
Values sent between devices are 32-bit elements; how exact they have to be, the bound alone decides.
A program may use at most 192 MiB of HBM per device.

```python
import math
import jax
import jax.numpy as jnp
from jax import lax

D = 8192
VOCAB = 128256
SLAB = 64
TOKS = 128
K = 32768
EX = 512


def mixed_field(key, shape_common, shape_whole):
    common = jax.random.normal(jax.random.fold_in(key, 11), shape_common, jnp.float32)
    private = jax.random.normal(jax.random.fold_in(key, 12), shape_whole, jnp.float32)
    values = (common[None] + private) * 0.7071
    return jnp.clip(values, -8.0, 8.0)


def draw_activations(key, part):
    return mixed_field(key, (TOKS, D), (EX, TOKS, D)).astype(jnp.bfloat16)


def draw_cotangents(key, part):
    return mixed_field(key, (TOKS, SLAB), (EX, TOKS, SLAB)).astype(jnp.bfloat16)


def draw_token_ids(key, part):
    lengths = jax.random.randint(jax.random.fold_in(key, 21), (EX,), TOKS // 4, TOKS + 1)
    token_values = jax.random.randint(jax.random.fold_in(key, 22), (EX, TOKS), 1, VOCAB)
    positions = jnp.arange(TOKS, dtype=jnp.int32)[None, :]
    return jnp.where(positions < lengths[:, None], token_values, 0).astype(jnp.int32)


def draw_signs(key, part):
    coins = jax.random.randint(jax.random.fold_in(key, 31), (SLAB, D), 0, 2)
    return (2 * coins - 1).astype(jnp.int32)


def draw_select(key, part):
    shuffled = jax.random.permutation(jax.random.fold_in(key, 41), SLAB * D - 2) + 1
    chosen = jnp.concatenate([shuffled[:K - 2].astype(jnp.int32), jnp.array([0, SLAB * D - 1], jnp.int32)])
    order = jax.random.permutation(jax.random.fold_in(key, 42), K)
    return chosen[order].astype(jnp.int32)


def setup_inputs(seed: int = 0) -> dict:
    streams_of = jax.random.split(jax.random.key(seed), 6)
    activations = draw_activations(jax.random.fold_in(streams_of[5], 71), 0)
    cotangents = draw_cotangents(jax.random.fold_in(streams_of[5], 71), 0)
    token_ids = draw_token_ids(jax.random.fold_in(streams_of[5], 71), 0)
    signs = draw_signs(jax.random.fold_in(streams_of[5], 71), 0)
    select = draw_select(jax.random.fold_in(streams_of[5], 71), 0)
    return {"activations": activations, "cotangents": cotangents, "token_ids": token_ids, "signs": signs, "select": select}


def walsh_rows(values):
    lead_rows = values.shape[0]
    length = values.shape[1]
    half_width = 1
    while half_width < length:
        paired = values.reshape(lead_rows, length // (2 * half_width), 2, half_width)
        first = paired[:, :, 0, :]
        second = paired[:, :, 1, :]
        values = jnp.stack([first + second, first - second], axis=2).reshape(lead_rows, length)
        half_width = half_width * 2
    return values

def reference(activations, cotangents, token_ids, signs, select):
    group = math.gcd(EX, 8)
    live_mask = token_ids != 0
    masked = jnp.where(live_mask[:, :, None], cotangents, jnp.zeros((), cotangents.dtype))
    flip_sign = signs.astype(jnp.float32).reshape(-1)

    def one_group(pair):
        acts, cots = pair
        gradient = jnp.einsum('etr,etc->erc', cots.astype(jnp.float32), acts.astype(jnp.float32), precision=lax.Precision.HIGHEST) * (1.0 / math.sqrt(TOKS))
        flipped = gradient.reshape(group, SLAB * D) * flip_sign[None, :]
        transformed = walsh_rows(flipped)
        return jnp.take(transformed, select, axis=1) / math.sqrt(SLAB * D)
    grouped = lax.map(one_group, (activations.reshape(EX // group, group, TOKS, D), masked.reshape(EX // group, group, TOKS, SLAB)))
    features = grouped.reshape(EX, K)
    gram = jnp.dot(features, features.T, precision=lax.Precision.HIGHEST, preferred_element_type=jnp.float32) / K
    return (features, gram)
```

```python
import functools

import jax
import jax.numpy as jnp
from jax import lax
from jax.experimental import pallas as pl
from jax.experimental.pallas import tpu as pltpu
from jax.sharding import PartitionSpec as P

LANES = 128
GROUP = 8


def walsh_table(table_order):
    row_index = lax.broadcasted_iota(jnp.int32, (table_order, table_order), 0)
    column_index = lax.broadcasted_iota(jnp.int32, (table_order, table_order), 1)
    common_bits = row_index & column_index
    parity = jnp.zeros((table_order, table_order), jnp.int32)
    for bit_index in range(table_order.bit_length() - 1):
        parity = parity ^ common_bits >> bit_index & 1
    return (1 - 2 * parity).astype(jnp.float32)


def split_two(value):
    high = value.astype(jnp.bfloat16)
    low = (value - high.astype(jnp.float32)).astype(jnp.bfloat16)
    return high, low


def mix_kernel(cots_ref, acts_ref, signs_ref, table_ref, out_ref, held):
    slab_rows = out_ref.shape[0]
    blocks = out_ref.shape[2] // LANES
    flip = signs_ref[...].astype(jnp.float32)
    for e in range(GROUP):
        gradient = jnp.dot(cots_ref[e], acts_ref[e], preferred_element_type=jnp.float32)
        high, low = split_two(gradient * flip)
        mixed = jnp.dot(
            table_ref[...], jnp.concatenate([high, low], axis=0), preferred_element_type=jnp.float32
        )
        for c in range(blocks):
            held[pl.ds((c * GROUP + e) * slab_rows, slab_rows), :] = mixed[:, c * LANES:(c + 1) * LANES]
    for r in range(slab_rows):
        for c in range(blocks):
            out_ref[r, :, c * LANES:(c + 1) * LANES] = held[
                pl.ds(c * GROUP * slab_rows + r, GROUP, stride=slab_rows), :
            ]


def mix_rows(cots, acts, signs, table):
    count_ex, slab_rows, toks = cots.shape
    width = acts.shape[2]
    block = min(width, 1024)
    return pl.pallas_call(
        mix_kernel,
        grid=(width // block, count_ex // GROUP),
        in_specs=[
            pl.BlockSpec((GROUP, slab_rows, toks), lambda c, e: (e, 0, 0)),
            pl.BlockSpec((GROUP, toks, block), lambda c, e: (e, 0, c)),
            pl.BlockSpec((slab_rows, block), lambda c, e: (0, c)),
            pl.BlockSpec(table.shape, lambda c, e: (0, 0)),
        ],
        out_specs=pl.BlockSpec((slab_rows, GROUP, block), lambda c, e: (0, e, c)),
        out_shape=jax.ShapeDtypeStruct((slab_rows, count_ex, width), jnp.float32),
        scratch_shapes=[pltpu.VMEM((GROUP * slab_rows * block // LANES, LANES), jnp.float32)],
    )(cots, acts, signs, table)


def pick_kernel(steps, rows_ref, mixed_ref, table_ref, upper_ref, weight_ref, out_ref, values, pieces, picked):
    step = pl.program_id(0)
    count_ex, width = mixed_ref.shape[2], mixed_ref.shape[3]
    blocks = width // LANES
    chunk = out_ref.shape[1]

    @pl.when(step < steps)
    def _():
        for half in range(2):
            for i in range(count_ex // 16):
                part = [
                    mixed_ref[half, 0, i * 16:(i + 1) * 16, a * LANES:(a + 1) * LANES] for a in range(blocks)
                ]
                span = 1
                while span < blocks:
                    part = [
                        part[a] + part[a + span] if a & span == 0 else part[a - span] - part[a]
                        for a in range(blocks)
                    ]
                    span *= 2
                row = half * count_ex + i * 16
                for a in range(blocks):
                    high, low = split_two(part[a])
                    pieces[row:row + 16, 2 * a * LANES:(2 * a + 1) * LANES] = high
                    pieces[row:row + 16, (2 * a + 1) * LANES:(2 * a + 2) * LANES] = low
        base = pl.multiple_of(step * width, LANES)
        for a in range(blocks):
            values[pl.ds(base + a * LANES, LANES), :] = lax.dot_general(
                table_ref[...],
                pieces[:, 2 * a * LANES:(2 * a + 2) * LANES],
                (((1,), (1,)), ((), ())),
                preferred_element_type=jnp.float32,
            )

    @pl.when(step >= steps)
    def _():
        start = (step - steps) * chunk

        def pick(i, carry):
            first = pl.multiple_of(i * 32, 32)
            taken = [values[pl.ds(rows_ref[start + first + j], 1), :] for j in range(32)]
            for j in range(32):
                picked[pl.ds(first + j, 1), :] = taken[j]
            return carry

        lax.fori_loop(0, chunk // 32, pick, 0)
        turned = picked[...].T
        out_ref[...] = jnp.where(upper_ref[...] > 0, turned[count_ex:], turned[:count_ex]) * weight_ref[...]


def pick_features(rows, mixed, table, upper, weight):
    slab_rows, count_ex, width = mixed.shape
    count = rows.shape[0]
    steps = slab_rows // 2
    chunk = min(count, 1024)
    halves = mixed.reshape(2, steps, count_ex, width)
    return pl.pallas_call(
        functools.partial(pick_kernel, steps),
        grid_spec=pltpu.PrefetchScalarGridSpec(
            num_scalar_prefetch=1,
            grid=(steps + count // chunk,),
            in_specs=[
                pl.BlockSpec((2, 1, count_ex, width), lambda s, rows: (0, jnp.minimum(s, steps - 1), 0, 0)),
                pl.BlockSpec(table.shape, lambda s, rows: (0, 0)),
                pl.BlockSpec((1, chunk), lambda s, rows: (0, jnp.maximum(s - steps, 0))),
                pl.BlockSpec((1, chunk), lambda s, rows: (0, jnp.maximum(s - steps, 0))),
            ],
            out_specs=pl.BlockSpec((count_ex, chunk), lambda s, rows: (0, jnp.maximum(s - steps, 0))),
            scratch_shapes=[
                pltpu.VMEM((steps * width, LANES), jnp.float32),
                pltpu.VMEM((2 * count_ex, 2 * width), jnp.bfloat16),
                pltpu.VMEM((chunk, LANES), jnp.float32),
            ],
        ),
        out_shape=jax.ShapeDtypeStruct((count_ex, count), jnp.float32),
        compiler_params=pltpu.CompilerParams(vmem_limit_bytes=60 * 1024 * 1024),
    )(rows, halves, table, upper, weight)


def body(activations, cotangents, token_ids, signs, select):
    local_width = activations.shape[2]
    toks = activations.shape[1]
    slab_rows = cotangents.shape[2]
    section_count = lax.axis_size("param")
    width = local_width * section_count
    live_mask = token_ids != 0
    masked = jnp.where(live_mask[:, :, None], cotangents, jnp.zeros((), cotangents.dtype))
    row_table = walsh_table(slab_rows).astype(jnp.bfloat16)
    lane_table = walsh_table(LANES).astype(jnp.bfloat16)
    mixed = mix_rows(
        jnp.swapaxes(masked, 1, 2), activations, signs, jnp.concatenate([row_table, row_table], axis=1)
    )
    factor = 1.0 / float(toks * slab_rows * width) ** 0.5
    my_index = lax.axis_index("param")
    column = select % width
    row = select // width
    shared = column // local_width & my_index
    parity = jnp.zeros_like(shared)
    for bit_index in range(section_count.bit_length() - 1):
        parity = parity ^ shared >> bit_index & 1
    weight = (1 - 2 * parity).astype(jnp.float32) * factor
    half_rows = slab_rows // 2
    rows = row % half_rows * local_width + column % local_width
    upper = (row // half_rows).astype(jnp.float32)
    partial_term = pick_features(
        rows, mixed, jnp.concatenate([lane_table, lane_table], axis=1), upper[None, :], weight[None, :]
    )
    features = lax.psum_scatter(partial_term, "param", scatter_dimension=1, tiled=True)
    swapped = lax.all_to_all(features, "ex", split_axis=1, concat_axis=0, tiled=True)
    tile = lax.dot_general(
        swapped, swapped, (((1,), (1,)), ((), ())), precision=lax.Precision.HIGHEST
    )
    tile_block = lax.psum_scatter(tile, "ex", scatter_dimension=0, tiled=True)
    gram = lax.psum(tile_block, "param") / select.shape[0]
    return (features, gram)


def solution(mesh):
    return jax.shard_map(
        body,
        mesh=mesh,
        in_specs=(
            P("ex", None, "param"),
            P("ex", None, None),
            P("ex", None),
            P(None, "param"),
            P(),
        ),
        out_specs=(P("ex", "param"), P("ex", None)),
        check_vma=False,
    )
```

```python
import functools

import jax
import jax.numpy as jnp
from jax import lax
from jax.experimental import pallas as pl
from jax.experimental.pallas import tpu as pltpu
from jax.sharding import PartitionSpec as P

LANES = 128
GROUP = 8


def walsh_table(table_order):
    row_index = lax.broadcasted_iota(jnp.int32, (table_order, table_order), 0)
    column_index = lax.broadcasted_iota(jnp.int32, (table_order, table_order), 1)
    common_bits = row_index & column_index
    parity = jnp.zeros((table_order, table_order), jnp.int32)
    for bit_index in range(table_order.bit_length() - 1):
        parity = parity ^ common_bits >> bit_index & 1
    return (1 - 2 * parity).astype(jnp.float32)


def split_two(value):
    high = value.astype(jnp.bfloat16)
    low = (value - high.astype(jnp.float32)).astype(jnp.bfloat16)
    return high, low


def mix_kernel(cots_ref, acts_ref, signs_ref, table_ref, out_ref, held):
    slab_rows = out_ref.shape[0]
    blocks = out_ref.shape[2] // LANES
    flip = signs_ref[...].astype(jnp.float32)
    for e in range(GROUP):
        gradient = jnp.dot(cots_ref[e], acts_ref[e], preferred_element_type=jnp.float32)
        high, low = split_two(gradient * flip)
        mixed = jnp.dot(
            table_ref[...], jnp.concatenate([high, low], axis=0), preferred_element_type=jnp.float32
        )
        for c in range(blocks):
            held[pl.ds((c * GROUP + e) * slab_rows, slab_rows), :] = mixed[:, c * LANES:(c + 1) * LANES]
    for r in range(slab_rows):
        for c in range(blocks):
            out_ref[r, :, c * LANES:(c + 1) * LANES] = held[
                pl.ds(c * GROUP * slab_rows + r, GROUP, stride=slab_rows), :
            ]


def mix_rows(cots, acts, signs, table):
    count_ex, slab_rows, toks = cots.shape
    width = acts.shape[2]
    block = min(width, 1024)
    return pl.pallas_call(
        mix_kernel,
        grid=(width // block, count_ex // GROUP),
        in_specs=[
            pl.BlockSpec((GROUP, slab_rows, toks), lambda c, e: (e, 0, 0)),
            pl.BlockSpec((GROUP, toks, block), lambda c, e: (e, 0, c)),
            pl.BlockSpec((slab_rows, block), lambda c, e: (0, c)),
            pl.BlockSpec(table.shape, lambda c, e: (0, 0)),
        ],
        out_specs=pl.BlockSpec((slab_rows, GROUP, block), lambda c, e: (0, e, c)),
        out_shape=jax.ShapeDtypeStruct((slab_rows, count_ex, width), jnp.float32),
        scratch_shapes=[pltpu.VMEM((GROUP * slab_rows * block // LANES, LANES), jnp.float32)],
    )(cots, acts, signs, table)


def pick_kernel(steps, rows_ref, mixed_ref, table_ref, upper_ref, weight_ref, out_ref, values, pieces, picked):
    step = pl.program_id(0)
    count_ex, width = mixed_ref.shape[2], mixed_ref.shape[3]
    blocks = width // LANES
    chunk = out_ref.shape[1]

    @pl.when(step < steps)
    def _():
        for half in range(2):
            for i in range(count_ex // 16):
                part = [
                    mixed_ref[half, 0, i * 16:(i + 1) * 16, a * LANES:(a + 1) * LANES] for a in range(blocks)
                ]
                span = 1
                while span < blocks:
                    part = [
                        part[a] + part[a + span] if a & span == 0 else part[a - span] - part[a]
                        for a in range(blocks)
                    ]
                    span *= 2
                row = half * count_ex + i * 16
                for a in range(blocks):
                    high, low = split_two(part[a])
                    pieces[row:row + 16, 2 * a * LANES:(2 * a + 1) * LANES] = high
                    pieces[row:row + 16, (2 * a + 1) * LANES:(2 * a + 2) * LANES] = low
        base = pl.multiple_of(step * width, LANES)
        for a in range(blocks):
            values[pl.ds(base + a * LANES, LANES), :] = lax.dot_general(
                table_ref[...],
                pieces[:, 2 * a * LANES:(2 * a + 2) * LANES],
                (((1,), (1,)), ((), ())),
                preferred_element_type=jnp.float32,
            )

    @pl.when(step >= steps)
    def _():
        start = (step - steps) * chunk

        def pick(i, carry):
            first = pl.multiple_of(i * 32, 32)
            taken = [values[pl.ds(rows_ref[start + first + j], 1), :] for j in range(32)]
            for j in range(32):
                picked[pl.ds(first + j, 1), :] = taken[j]
            return carry

        lax.fori_loop(0, chunk // 32, pick, 0)
        turned = picked[...].T
        out_ref[...] = jnp.where(upper_ref[...] > 0, turned[count_ex:], turned[:count_ex]) * weight_ref[...]


def pick_features(rows, mixed, table, upper, weight):
    slab_rows, count_ex, width = mixed.shape
    count = rows.shape[0]
    steps = slab_rows // 2
    chunk = min(count, 1024)
    halves = mixed.reshape(2, steps, count_ex, width)
    return pl.pallas_call(
        functools.partial(pick_kernel, steps),
        grid_spec=pltpu.PrefetchScalarGridSpec(
            num_scalar_prefetch=1,
            grid=(steps + count // chunk,),
            in_specs=[
                pl.BlockSpec((2, 1, count_ex, width), lambda s, rows: (0, jnp.minimum(s, steps - 1), 0, 0)),
                pl.BlockSpec(table.shape, lambda s, rows: (0, 0)),
                pl.BlockSpec((1, chunk), lambda s, rows: (0, jnp.maximum(s - steps, 0))),
                pl.BlockSpec((1, chunk), lambda s, rows: (0, jnp.maximum(s - steps, 0))),
            ],
            out_specs=pl.BlockSpec((count_ex, chunk), lambda s, rows: (0, jnp.maximum(s - steps, 0))),
            scratch_shapes=[
                pltpu.VMEM((steps * width, LANES), jnp.float32),
                pltpu.VMEM((2 * count_ex, 2 * width), jnp.bfloat16),
                pltpu.VMEM((chunk, LANES), jnp.float32),
            ],
        ),
        out_shape=jax.ShapeDtypeStruct((count_ex, count), jnp.float32),
        compiler_params=pltpu.CompilerParams(vmem_limit_bytes=60 * 1024 * 1024),
    )(rows, halves, table, upper, weight)


def gram_kernel(sections, groups, count, tile_ref, out_ref, first, total, second, done, third, s1, r1, s2, r2, s3, r3):
    mine, place = lax.axis_index("param"), lax.axis_index("ex")
    height, width = out_ref.shape[0], total.shape[1]
    barrier = pltpu.get_barrier_semaphore()
    for d in range(1, sections):
        pl.semaphore_signal(
            barrier, inc=1, device_id={"param": lax.rem(mine + d, sections)}, device_id_type=pl.DeviceIdType.MESH
        )
    for d in range(1, groups):
        pl.semaphore_signal(
            barrier, inc=1, device_id={"ex": lax.rem(place + d, groups)}, device_id_type=pl.DeviceIdType.MESH
        )
    pl.semaphore_wait(barrier, sections + groups - 2)

    def send(axis, target, source, landing, send_sem, recv_sem, d):
        copy = pltpu.make_async_remote_copy(
            src_ref=source,
            dst_ref=landing.at[d - 1],
            send_sem=send_sem.at[d - 1],
            recv_sem=recv_sem.at[d - 1],
            device_id={axis: target},
            device_id_type=pl.DeviceIdType.MESH,
        )
        copy.start()
        return copy

    def columns(index):
        return pl.ds(pl.multiple_of(index * width, width), width)

    def lines(index):
        return pl.ds(pl.multiple_of(index * height, height), height)

    copies = []
    for d in range(1, sections):
        target = lax.rem(mine + d, sections)
        copies.append(send("param", target, tile_ref.at[:, columns(target)], first, s1, r1, d))
    total[...] = tile_ref[:, columns(mine)]
    for d, copy in enumerate(copies):
        copy.wait()
        total[...] += first[d]
    copies = []
    for d in range(1, groups):
        target = lax.rem(place + d, groups)
        copies.append(send("ex", target, total.at[lines(target), :], second, s2, r2, d))
    result = total[lines(place), :]
    for d, copy in enumerate(copies):
        copy.wait()
        result = result + second[d]
    done[...] = result / count
    copies = []
    for d in range(1, sections):
        copies.append(send("param", lax.rem(mine + d, sections), done, third, s3, r3, d))
    out_ref[:, columns(mine)] = done[...]
    for d, copy in enumerate(copies):
        copy.wait()
        out_ref[:, columns(lax.rem(mine + sections - d - 1, sections))] = third[d]


def reduce_gram(tile, count):
    sections, groups = lax.axis_size("param"), lax.axis_size("ex")
    examples = tile.shape[0]
    height, width = examples // groups, examples // sections
    dma = pltpu.SemaphoreType.DMA
    return pl.pallas_call(
        functools.partial(gram_kernel, sections, groups, count),
        out_shape=jax.ShapeDtypeStruct((height, examples), jnp.float32),
        in_specs=[pl.BlockSpec(memory_space=pltpu.VMEM)],
        out_specs=pl.BlockSpec(memory_space=pltpu.VMEM),
        scratch_shapes=[
            pltpu.VMEM((sections - 1, examples, width), jnp.float32),
            pltpu.VMEM((examples, width), jnp.float32),
            pltpu.VMEM((groups - 1, height, width), jnp.float32),
            pltpu.VMEM((height, width), jnp.float32),
            pltpu.VMEM((sections - 1, height, width), jnp.float32),
            dma((sections - 1,)),
            dma((sections - 1,)),
            dma((groups - 1,)),
            dma((groups - 1,)),
            dma((sections - 1,)),
            dma((sections - 1,)),
        ],
        compiler_params=pltpu.CompilerParams(collective_id=1, has_side_effects=True),
    )(tile)


def body(activations, cotangents, token_ids, signs, select):
    local_width = activations.shape[2]
    toks = activations.shape[1]
    slab_rows = cotangents.shape[2]
    section_count = lax.axis_size("param")
    width = local_width * section_count
    live_mask = token_ids != 0
    masked = jnp.where(live_mask[:, :, None], cotangents, jnp.zeros((), cotangents.dtype))
    row_table = walsh_table(slab_rows).astype(jnp.bfloat16)
    lane_table = walsh_table(LANES).astype(jnp.bfloat16)
    mixed = mix_rows(
        jnp.swapaxes(masked, 1, 2), activations, signs, jnp.concatenate([row_table, row_table], axis=1)
    )
    factor = 1.0 / float(toks * slab_rows * width) ** 0.5
    my_index = lax.axis_index("param")
    column = select % width
    row = select // width
    shared = column // local_width & my_index
    parity = jnp.zeros_like(shared)
    for bit_index in range(section_count.bit_length() - 1):
        parity = parity ^ shared >> bit_index & 1
    weight = (1 - 2 * parity).astype(jnp.float32) * factor
    half_rows = slab_rows // 2
    rows = row % half_rows * local_width + column % local_width
    upper = (row // half_rows).astype(jnp.float32)
    partial_term = pick_features(
        rows, mixed, jnp.concatenate([lane_table, lane_table], axis=1), upper[None, :], weight[None, :]
    )
    features = lax.psum_scatter(partial_term, "param", scatter_dimension=1, tiled=True)
    swapped = lax.all_to_all(features, "ex", split_axis=1, concat_axis=0, tiled=True)
    tile = lax.dot_general(
        swapped, swapped, (((1,), (1,)), ((), ())), precision=lax.Precision.HIGHEST
    )
    gram = reduce_gram(tile, select.shape[0])
    return (features, gram)


def solution(mesh):
    return jax.shard_map(
        body,
        mesh=mesh,
        in_specs=(
            P("ex", None, "param"),
            P("ex", None, None),
            P("ex", None),
            P(None, "param"),
            P(),
        ),
        out_specs=(P("ex", "param"), P("ex", None)),
        check_vma=False,
    )
```

```python
import functools

import jax
import jax.numpy as jnp
from jax import lax
from jax.experimental import pallas as pl
from jax.experimental.pallas import tpu as pltpu
from jax.sharding import PartitionSpec as P

LANES = 128
GROUP = 8


def walsh_table(table_order):
    row_index = lax.broadcasted_iota(jnp.int32, (table_order, table_order), 0)
    column_index = lax.broadcasted_iota(jnp.int32, (table_order, table_order), 1)
    common_bits = row_index & column_index
    parity = jnp.zeros((table_order, table_order), jnp.int32)
    for bit_index in range(table_order.bit_length() - 1):
        parity = parity ^ common_bits >> bit_index & 1
    return (1 - 2 * parity).astype(jnp.float32)


def split_two(value):
    high = value.astype(jnp.bfloat16)
    low = (value - high.astype(jnp.float32)).astype(jnp.bfloat16)
    return high, low


def mix_kernel(cots_ref, acts_ref, signs_ref, table_ref, out_ref, held):
    slab_rows = out_ref.shape[0]
    blocks = out_ref.shape[2] // LANES
    flip = signs_ref[...].astype(jnp.float32)
    for e in range(GROUP):
        gradient = jnp.dot(cots_ref[e], acts_ref[e], preferred_element_type=jnp.float32)
        high, low = split_two(gradient * flip)
        mixed = jnp.dot(
            table_ref[...], jnp.concatenate([high, low], axis=0), preferred_element_type=jnp.float32
        )
        for c in range(blocks):
            held[pl.ds((c * GROUP + e) * slab_rows, slab_rows), :] = mixed[:, c * LANES:(c + 1) * LANES]
    for r in range(slab_rows):
        for c in range(blocks):
            out_ref[r, :, c * LANES:(c + 1) * LANES] = held[
                pl.ds(c * GROUP * slab_rows + r, GROUP, stride=slab_rows), :
            ]


def mix_rows(cots, acts, signs, table):
    count_ex, slab_rows, toks = cots.shape
    width = acts.shape[2]
    block = min(width, 1024)
    return pl.pallas_call(
        mix_kernel,
        grid=(width // block, count_ex // GROUP),
        in_specs=[
            pl.BlockSpec((GROUP, slab_rows, toks), lambda c, e: (e, 0, 0)),
            pl.BlockSpec((GROUP, toks, block), lambda c, e: (e, 0, c)),
            pl.BlockSpec((slab_rows, block), lambda c, e: (0, c)),
            pl.BlockSpec(table.shape, lambda c, e: (0, 0)),
        ],
        out_specs=pl.BlockSpec((slab_rows, GROUP, block), lambda c, e: (0, e, c)),
        out_shape=jax.ShapeDtypeStruct((slab_rows, count_ex, width), jnp.float32),
        scratch_shapes=[pltpu.VMEM((GROUP * slab_rows * block // LANES, LANES), jnp.float32)],
    )(cots, acts, signs, table)


def pick_kernel(steps, rows_ref, mixed_ref, table_ref, upper_ref, weight_ref, out_ref, values, pieces, picked):
    step = pl.program_id(0)
    count_ex, width = mixed_ref.shape[2], mixed_ref.shape[3]
    blocks = width // LANES
    chunk = out_ref.shape[1]

    @pl.when(step < steps)
    def _():
        for half in range(2):
            for i in range(count_ex // 16):
                part = [
                    mixed_ref[half, 0, i * 16:(i + 1) * 16, a * LANES:(a + 1) * LANES] for a in range(blocks)
                ]
                span = 1
                while span < blocks:
                    part = [
                        part[a] + part[a + span] if a & span == 0 else part[a - span] - part[a]
                        for a in range(blocks)
                    ]
                    span *= 2
                row = half * count_ex + i * 16
                for a in range(blocks):
                    high, low = split_two(part[a])
                    pieces[row:row + 16, 2 * a * LANES:(2 * a + 1) * LANES] = high
                    pieces[row:row + 16, (2 * a + 1) * LANES:(2 * a + 2) * LANES] = low
        base = pl.multiple_of(step * width, LANES)
        for a in range(blocks):
            values[pl.ds(base + a * LANES, LANES), :] = lax.dot_general(
                table_ref[...],
                pieces[:, 2 * a * LANES:(2 * a + 2) * LANES],
                (((1,), (1,)), ((), ())),
                preferred_element_type=jnp.float32,
            )

    @pl.when(step >= steps)
    def _():
        start = (step - steps) * chunk

        def pick(i, carry):
            first = pl.multiple_of(i * 32, 32)
            taken = [values[pl.ds(rows_ref[start + first + j], 1), :] for j in range(32)]
            for j in range(32):
                picked[pl.ds(first + j, 1), :] = taken[j]
            return carry

        lax.fori_loop(0, chunk // 32, pick, 0)
        turned = picked[...].T
        out_ref[...] = jnp.where(upper_ref[...] > 0, turned[count_ex:], turned[:count_ex]) * weight_ref[...]


def pick_features(rows, mixed, table, upper, weight):
    slab_rows, count_ex, width = mixed.shape
    count = rows.shape[0]
    steps = slab_rows // 2
    chunk = min(count, 1024)
    halves = mixed.reshape(2, steps, count_ex, width)
    return pl.pallas_call(
        functools.partial(pick_kernel, steps),
        grid_spec=pltpu.PrefetchScalarGridSpec(
            num_scalar_prefetch=1,
            grid=(steps + count // chunk,),
            in_specs=[
                pl.BlockSpec((2, 1, count_ex, width), lambda s, rows: (0, jnp.minimum(s, steps - 1), 0, 0)),
                pl.BlockSpec(table.shape, lambda s, rows: (0, 0)),
                pl.BlockSpec((1, chunk), lambda s, rows: (0, jnp.maximum(s - steps, 0))),
                pl.BlockSpec((1, chunk), lambda s, rows: (0, jnp.maximum(s - steps, 0))),
            ],
            out_specs=pl.BlockSpec((count_ex, chunk), lambda s, rows: (0, jnp.maximum(s - steps, 0))),
            scratch_shapes=[
                pltpu.VMEM((steps * width, LANES), jnp.float32),
                pltpu.VMEM((2 * count_ex, 2 * width), jnp.bfloat16),
                pltpu.VMEM((chunk, LANES), jnp.float32),
            ],
        ),
        out_shape=jax.ShapeDtypeStruct((count_ex, count), jnp.float32),
        compiler_params=pltpu.CompilerParams(vmem_limit_bytes=60 * 1024 * 1024),
    )(rows, halves, table, upper, weight)


def share_kernel(
    rows_of_y, groups, part_ref, out_ref, tile_ref, near, sums, far, whole, near_s, near_r, far_s, far_r, ex_s, ex_r
):
    mine, place = lax.axis_index("param"), lax.axis_index("ex")
    my_y, my_core = mine // 2, lax.rem(mine, 2)
    height, block = out_ref.shape
    width = block // groups
    barrier = pltpu.get_barrier_semaphore()
    mesh_type = pl.DeviceIdType.MESH

    def owner(dy, core):
        return lax.rem(my_y + dy, rows_of_y) * 2 + core

    pl.semaphore_signal(barrier, inc=1, device_id={"param": owner(0, 1 - my_core)}, device_id_type=mesh_type)
    for dy in range(1, rows_of_y):
        pl.semaphore_signal(barrier, inc=1, device_id={"param": owner(dy, my_core)}, device_id_type=mesh_type)
    for d in range(1, groups):
        pl.semaphore_signal(
            barrier, inc=1, device_id={"ex": lax.rem(place + d, groups)}, device_id_type=mesh_type
        )
    pl.semaphore_wait(barrier, rows_of_y + groups - 1)

    def part(dy, core, slot):
        start = owner(dy, core) * block + slot * width
        return (slice(None), pl.ds(pl.multiple_of(start, width), width))

    def send(target, source, landing, send_sem, recv_sem):
        copy = pltpu.make_async_remote_copy(
            src_ref=source,
            dst_ref=landing,
            send_sem=send_sem,
            recv_sem=recv_sem,
            device_id=target,
            device_id_type=mesh_type,
        )
        copy.start()
        return copy

    order = list(range(1, groups)) + [0]
    slots = {m: lax.rem(place + m, groups) for m in order}
    offsets = list(range(1, rows_of_y)) + [0]
    near_copies, far_copies, ex_copies = {}, {}, {}
    for m in order:
        for dy in offsets:
            n = m * rows_of_y + dy
            near_copies[m, dy] = send(
                {"param": owner(0, 1 - my_core)},
                part_ref.at[part(dy, 1 - my_core, slots[m])],
                near.at[n],
                near_s.at[n],
                near_r.at[n],
            )
    for m in order:
        for dy in offsets:
            near_copies[m, dy].wait_recv()
            joined = part_ref[part(dy, my_core, slots[m])] + near[m * rows_of_y + dy]
            if dy == 0:
                out_ref[:, pl.ds(pl.multiple_of(slots[m] * width, width), width)] = joined
            else:
                n = m * (rows_of_y - 1) + dy - 1
                sums[n] = joined
                far_copies[m, dy] = send(
                    {"param": owner(dy, my_core)}, sums.at[n], far.at[n], far_s.at[n], far_r.at[n]
                )
    my_lines = pl.ds(pl.multiple_of(place * height, height), height)
    for m in order:
        here = pl.ds(pl.multiple_of(slots[m] * width, width), width)
        joined = out_ref[:, here]
        for dy in range(1, rows_of_y):
            far_copies[m, dy].wait_recv()
            joined = joined + far[m * (rows_of_y - 1) + dy - 1]
        out_ref[:, here] = joined
        if m == 0:
            whole[my_lines, :] = joined
        else:
            ex_copies[m] = send(
                {"ex": slots[m]}, out_ref.at[:, here], whole.at[my_lines, :], ex_s.at[m], ex_r.at[m]
            )
    for copy in near_copies.values():
        copy.wait_send()
    for copy in far_copies.values():
        copy.wait_send()
    for copy in ex_copies.values():
        copy.wait()
    tile_ref[...] = lax.dot_general(
        whole[...],
        whole[...],
        (((1,), (1,)), ((), ())),
        precision=lax.Precision.HIGHEST,
        preferred_element_type=jnp.float32,
    )


def share_features(partial_term):
    sections, groups = lax.axis_size("param"), lax.axis_size("ex")
    height, count = partial_term.shape
    rows_of_y = sections // 2
    block = count // sections
    width = block // groups
    examples = height * groups
    dma = pltpu.SemaphoreType.DMA
    near_count, far_count = groups * rows_of_y, groups * max(rows_of_y - 1, 1)
    vmem = pl.BlockSpec(memory_space=pltpu.VMEM)
    return pl.pallas_call(
        functools.partial(share_kernel, rows_of_y, groups),
        out_shape=(
            jax.ShapeDtypeStruct((height, block), jnp.float32),
            jax.ShapeDtypeStruct((examples, examples), jnp.float32),
        ),
        in_specs=[vmem],
        out_specs=(vmem, vmem),
        scratch_shapes=[
            pltpu.VMEM((near_count, height, width), jnp.float32),
            pltpu.VMEM((far_count, height, width), jnp.float32),
            pltpu.VMEM((far_count, height, width), jnp.float32),
            pltpu.VMEM((examples, width), jnp.float32),
            dma((near_count,)),
            dma((near_count,)),
            dma((far_count,)),
            dma((far_count,)),
            dma((groups,)),
            dma((groups,)),
        ],
        compiler_params=pltpu.CompilerParams(
            collective_id=2, has_side_effects=True, vmem_limit_bytes=60 * 1024 * 1024
        ),
    )(partial_term)


def gram_kernel(sections, groups, count, tile_ref, out_ref, first, total, second, done, third, s1, r1, s2, r2, s3, r3):
    mine, place = lax.axis_index("param"), lax.axis_index("ex")
    height, width = out_ref.shape[0], total.shape[1]
    barrier = pltpu.get_barrier_semaphore()
    for d in range(1, sections):
        pl.semaphore_signal(
            barrier, inc=1, device_id={"param": lax.rem(mine + d, sections)}, device_id_type=pl.DeviceIdType.MESH
        )
    for d in range(1, groups):
        pl.semaphore_signal(
            barrier, inc=1, device_id={"ex": lax.rem(place + d, groups)}, device_id_type=pl.DeviceIdType.MESH
        )
    pl.semaphore_wait(barrier, sections + groups - 2)

    def send(axis, target, source, landing, send_sem, recv_sem, d):
        copy = pltpu.make_async_remote_copy(
            src_ref=source,
            dst_ref=landing.at[d - 1],
            send_sem=send_sem.at[d - 1],
            recv_sem=recv_sem.at[d - 1],
            device_id={axis: target},
            device_id_type=pl.DeviceIdType.MESH,
        )
        copy.start()
        return copy

    def columns(index):
        return pl.ds(pl.multiple_of(index * width, width), width)

    def lines(index):
        return pl.ds(pl.multiple_of(index * height, height), height)

    copies = []
    for d in range(1, sections):
        target = lax.rem(mine + d, sections)
        copies.append(send("param", target, tile_ref.at[:, columns(target)], first, s1, r1, d))
    total[...] = tile_ref[:, columns(mine)]
    for d, copy in enumerate(copies):
        copy.wait()
        total[...] += first[d]
    copies = []
    for d in range(1, groups):
        target = lax.rem(place + d, groups)
        copies.append(send("ex", target, total.at[lines(target), :], second, s2, r2, d))
    result = total[lines(place), :]
    for d, copy in enumerate(copies):
        copy.wait()
        result = result + second[d]
    done[...] = result / count
    copies = []
    for d in range(1, sections):
        copies.append(send("param", lax.rem(mine + d, sections), done, third, s3, r3, d))
    out_ref[:, columns(mine)] = done[...]
    for d, copy in enumerate(copies):
        copy.wait()
        out_ref[:, columns(lax.rem(mine + sections - d - 1, sections))] = third[d]


def reduce_gram(tile, count):
    sections, groups = lax.axis_size("param"), lax.axis_size("ex")
    examples = tile.shape[0]
    height, width = examples // groups, examples // sections
    dma = pltpu.SemaphoreType.DMA
    return pl.pallas_call(
        functools.partial(gram_kernel, sections, groups, count),
        out_shape=jax.ShapeDtypeStruct((height, examples), jnp.float32),
        in_specs=[pl.BlockSpec(memory_space=pltpu.VMEM)],
        out_specs=pl.BlockSpec(memory_space=pltpu.VMEM),
        scratch_shapes=[
            pltpu.VMEM((sections - 1, examples, width), jnp.float32),
            pltpu.VMEM((examples, width), jnp.float32),
            pltpu.VMEM((groups - 1, height, width), jnp.float32),
            pltpu.VMEM((height, width), jnp.float32),
            pltpu.VMEM((sections - 1, height, width), jnp.float32),
            dma((sections - 1,)),
            dma((sections - 1,)),
            dma((groups - 1,)),
            dma((groups - 1,)),
            dma((sections - 1,)),
            dma((sections - 1,)),
        ],
        compiler_params=pltpu.CompilerParams(collective_id=1, has_side_effects=True),
    )(tile)


def body(activations, cotangents, token_ids, signs, select):
    local_width = activations.shape[2]
    toks = activations.shape[1]
    slab_rows = cotangents.shape[2]
    section_count = lax.axis_size("param")
    width = local_width * section_count
    live_mask = token_ids != 0
    masked = jnp.where(live_mask[:, :, None], cotangents, jnp.zeros((), cotangents.dtype))
    row_table = walsh_table(slab_rows).astype(jnp.bfloat16)
    lane_table = walsh_table(LANES).astype(jnp.bfloat16)
    mixed = mix_rows(
        jnp.swapaxes(masked, 1, 2), activations, signs, jnp.concatenate([row_table, row_table], axis=1)
    )
    factor = 1.0 / float(toks * slab_rows * width) ** 0.5
    my_index = lax.axis_index("param")
    column = select % width
    row = select // width
    shared = column // local_width & my_index
    parity = jnp.zeros_like(shared)
    for bit_index in range(section_count.bit_length() - 1):
        parity = parity ^ shared >> bit_index & 1
    weight = (1 - 2 * parity).astype(jnp.float32) * factor
    half_rows = slab_rows // 2
    rows = row % half_rows * local_width + column % local_width
    upper = (row // half_rows).astype(jnp.float32)
    partial_term = pick_features(
        rows, mixed, jnp.concatenate([lane_table, lane_table], axis=1), upper[None, :], weight[None, :]
    )
    features, tile = share_features(partial_term)
    gram = reduce_gram(tile, select.shape[0])
    return (features, gram)


def solution(mesh):
    return jax.shard_map(
        body,
        mesh=mesh,
        in_specs=(
            P("ex", None, "param"),
            P("ex", None, None),
            P("ex", None),
            P(None, "param"),
            P(),
        ),
        out_specs=(P("ex", "param"), P("ex", None)),
        check_vma=False,
    )
```

```python
import functools

import jax
import jax.numpy as jnp
from jax import lax
from jax.experimental import pallas as pl
from jax.experimental.pallas import tpu as pltpu
from jax.sharding import PartitionSpec as P

LANES = 128
GROUP = 8


def walsh_table(table_order):
    row_index = lax.broadcasted_iota(jnp.int32, (table_order, table_order), 0)
    column_index = lax.broadcasted_iota(jnp.int32, (table_order, table_order), 1)
    common_bits = row_index & column_index
    parity = jnp.zeros((table_order, table_order), jnp.int32)
    for bit_index in range(table_order.bit_length() - 1):
        parity = parity ^ common_bits >> bit_index & 1
    return (1 - 2 * parity).astype(jnp.float32)


def split_two(value):
    high = value.astype(jnp.bfloat16)
    low = (value - high.astype(jnp.float32)).astype(jnp.bfloat16)
    return high, low


def butterfly(part):
    span = 1
    while span < len(part):
        part = [
            part[a] + part[a + span] if a & span == 0 else part[a - span] - part[a] for a in range(len(part))
        ]
        span *= 2
    return part


def mix_kernel(cots_ref, acts_ref, signs_ref, apart_ref, out_ref, held):
    slab_rows, group, block = out_ref.shape
    toks = cots_ref.shape[2]
    spread = jnp.concatenate([cots_ref[0]] * group, axis=1) * apart_ref[...]
    held[...] = jnp.dot(
        spread, acts_ref[...].reshape(group * toks, block), preferred_element_type=jnp.float32
    )
    radix = 8
    for c in range(block // LANES):
        lanes = slice(c * LANES, (c + 1) * LANES)
        flip = signs_ref[:, lanes].astype(jnp.float32)
        for high in range(slab_rows // radix):
            rows = [high * radix + j for j in range(radix)]
            part = butterfly([
                held[r * group:(r + 1) * group, lanes] * jnp.broadcast_to(flip[r:r + 1], (group, LANES))
                for r in rows
            ])
            for r, value in zip(rows, part):
                held[r * group:(r + 1) * group, lanes] = value
        for low in range(radix):
            rows = list(range(low, slab_rows, radix))
            part = butterfly([held[r * group:(r + 1) * group, lanes] for r in rows])
            for r, value in zip(rows, part):
                out_ref[r, :, lanes] = value


def mix_rows(cots, acts, signs):
    count_ex, toks, slab_rows = cots.shape
    width = acts.shape[2]
    block = min(width, 1024)
    spread = cots.reshape(count_ex // GROUP, GROUP, toks, slab_rows).transpose(0, 3, 1, 2)
    spread = spread.reshape(count_ex // GROUP, slab_rows * GROUP, toks)
    shape = (slab_rows * GROUP, GROUP * toks)
    apart = lax.broadcasted_iota(jnp.int32, shape, 0) % GROUP == lax.broadcasted_iota(jnp.int32, shape, 1) // toks
    return pl.pallas_call(
        mix_kernel,
        grid=(width // block, count_ex // GROUP),
        in_specs=[
            pl.BlockSpec((1, slab_rows * GROUP, toks), lambda c, e: (e, 0, 0)),
            pl.BlockSpec((GROUP, toks, block), lambda c, e: (e, 0, c)),
            pl.BlockSpec((slab_rows, block), lambda c, e: (0, c)),
            pl.BlockSpec(shape, lambda c, e: (0, 0)),
        ],
        out_specs=pl.BlockSpec((slab_rows, GROUP, block), lambda c, e: (0, e, c)),
        out_shape=jax.ShapeDtypeStruct((slab_rows, count_ex, width), jnp.float32),
        scratch_shapes=[pltpu.VMEM((slab_rows * GROUP, block), jnp.float32)],
    )(spread, acts, signs, apart.astype(jnp.bfloat16))


def pick_kernel(steps, rows_ref, mixed_ref, table_ref, upper_ref, weight_ref, out_ref, values, pieces, picked):
    step = pl.program_id(0)
    count_ex, width = mixed_ref.shape[2], mixed_ref.shape[3]
    blocks = width // LANES
    chunk = out_ref.shape[1]

    @pl.when(step < steps)
    def _():
        for half in range(2):
            for i in range(count_ex // 16):
                part = [
                    mixed_ref[half, 0, i * 16:(i + 1) * 16, a * LANES:(a + 1) * LANES] for a in range(blocks)
                ]
                span = 1
                while span < blocks:
                    part = [
                        part[a] + part[a + span] if a & span == 0 else part[a - span] - part[a]
                        for a in range(blocks)
                    ]
                    span *= 2
                row = half * count_ex + i * 16
                for a in range(blocks):
                    high, low = split_two(part[a])
                    pieces[row:row + 16, 2 * a * LANES:(2 * a + 1) * LANES] = high
                    pieces[row:row + 16, (2 * a + 1) * LANES:(2 * a + 2) * LANES] = low
        base = pl.multiple_of(step * width, LANES)
        for a in range(blocks):
            values[pl.ds(base + a * LANES, LANES), :] = lax.dot_general(
                table_ref[...],
                pieces[:, 2 * a * LANES:(2 * a + 2) * LANES],
                (((1,), (1,)), ((), ())),
                preferred_element_type=jnp.float32,
            )

    @pl.when(step >= steps)
    def _():
        start = (step - steps) * chunk

        def pick(i, carry):
            first = pl.multiple_of(i * 32, 32)
            taken = [values[pl.ds(rows_ref[start + first + j], 1), :] for j in range(32)]
            for j in range(32):
                picked[pl.ds(first + j, 1), :] = taken[j]
            return carry

        lax.fori_loop(0, chunk // 32, pick, 0)
        turned = picked[...].T
        out_ref[...] = jnp.where(upper_ref[...] > 0, turned[count_ex:], turned[:count_ex]) * weight_ref[...]


def pick_features(rows, mixed, table, upper, weight):
    slab_rows, count_ex, width = mixed.shape
    count = rows.shape[0]
    steps = slab_rows // 2
    chunk = min(count, 1024)
    halves = mixed.reshape(2, steps, count_ex, width)
    return pl.pallas_call(
        functools.partial(pick_kernel, steps),
        grid_spec=pltpu.PrefetchScalarGridSpec(
            num_scalar_prefetch=1,
            grid=(steps + count // chunk,),
            in_specs=[
                pl.BlockSpec((2, 1, count_ex, width), lambda s, rows: (0, jnp.minimum(s, steps - 1), 0, 0)),
                pl.BlockSpec(table.shape, lambda s, rows: (0, 0)),
                pl.BlockSpec((1, chunk), lambda s, rows: (0, jnp.maximum(s - steps, 0))),
                pl.BlockSpec((1, chunk), lambda s, rows: (0, jnp.maximum(s - steps, 0))),
            ],
            out_specs=pl.BlockSpec((count_ex, chunk), lambda s, rows: (0, jnp.maximum(s - steps, 0))),
            scratch_shapes=[
                pltpu.VMEM((steps * width, LANES), jnp.float32),
                pltpu.VMEM((2 * count_ex, 2 * width), jnp.bfloat16),
                pltpu.VMEM((chunk, LANES), jnp.float32),
            ],
        ),
        out_shape=jax.ShapeDtypeStruct((count_ex, count), jnp.float32),
        compiler_params=pltpu.CompilerParams(vmem_limit_bytes=60 * 1024 * 1024),
    )(rows, halves, table, upper, weight)


def share_kernel(
    rows_of_y, groups, part_ref, out_ref, tile_ref, near, sums, far, whole, near_s, near_r, far_s, far_r, ex_s, ex_r
):
    mine, place = lax.axis_index("param"), lax.axis_index("ex")
    my_y, my_core = mine // 2, lax.rem(mine, 2)
    height, block = out_ref.shape
    width = block // groups
    barrier = pltpu.get_barrier_semaphore()
    mesh_type = pl.DeviceIdType.MESH

    def owner(dy, core):
        return lax.rem(my_y + dy, rows_of_y) * 2 + core

    pl.semaphore_signal(barrier, inc=1, device_id={"param": owner(0, 1 - my_core)}, device_id_type=mesh_type)
    for dy in range(1, rows_of_y):
        pl.semaphore_signal(barrier, inc=1, device_id={"param": owner(dy, my_core)}, device_id_type=mesh_type)
    for d in range(1, groups):
        pl.semaphore_signal(
            barrier, inc=1, device_id={"ex": lax.rem(place + d, groups)}, device_id_type=mesh_type
        )
    pl.semaphore_wait(barrier, rows_of_y + groups - 1)

    def part(dy, core, slot):
        start = owner(dy, core) * block + slot * width
        return (slice(None), pl.ds(pl.multiple_of(start, width), width))

    def send(target, source, landing, send_sem, recv_sem):
        copy = pltpu.make_async_remote_copy(
            src_ref=source,
            dst_ref=landing,
            send_sem=send_sem,
            recv_sem=recv_sem,
            device_id=target,
            device_id_type=mesh_type,
        )
        copy.start()
        return copy

    order = list(range(1, groups)) + [0]
    slots = {m: lax.rem(place + m, groups) for m in order}
    offsets = list(range(1, rows_of_y)) + [0]
    near_copies, far_copies, ex_copies = {}, {}, {}
    for m in order:
        for dy in offsets:
            n = m * rows_of_y + dy
            near_copies[m, dy] = send(
                {"param": owner(0, 1 - my_core)},
                part_ref.at[part(dy, 1 - my_core, slots[m])],
                near.at[n],
                near_s.at[n],
                near_r.at[n],
            )
    for m in order:
        for dy in offsets:
            near_copies[m, dy].wait_recv()
            joined = part_ref[part(dy, my_core, slots[m])] + near[m * rows_of_y + dy]
            if dy == 0:
                out_ref[:, pl.ds(pl.multiple_of(slots[m] * width, width), width)] = joined
            else:
                n = m * (rows_of_y - 1) + dy - 1
                sums[n] = joined
                far_copies[m, dy] = send(
                    {"param": owner(dy, my_core)}, sums.at[n], far.at[n], far_s.at[n], far_r.at[n]
                )
    my_lines = pl.ds(pl.multiple_of(place * height, height), height)
    for m in order:
        here = pl.ds(pl.multiple_of(slots[m] * width, width), width)
        joined = out_ref[:, here]
        for dy in range(1, rows_of_y):
            far_copies[m, dy].wait_recv()
            joined = joined + far[m * (rows_of_y - 1) + dy - 1]
        out_ref[:, here] = joined
        if m == 0:
            whole[my_lines, :] = joined
        else:
            ex_copies[m] = send(
                {"ex": slots[m]}, out_ref.at[:, here], whole.at[my_lines, :], ex_s.at[m], ex_r.at[m]
            )
    for copy in near_copies.values():
        copy.wait_send()
    for copy in far_copies.values():
        copy.wait_send()
    for copy in ex_copies.values():
        copy.wait()
    tile_ref[...] = lax.dot_general(
        whole[...],
        whole[...],
        (((1,), (1,)), ((), ())),
        precision=lax.Precision.HIGHEST,
        preferred_element_type=jnp.float32,
    )


def share_features(partial_term):
    sections, groups = lax.axis_size("param"), lax.axis_size("ex")
    height, count = partial_term.shape
    rows_of_y = sections // 2
    block = count // sections
    width = block // groups
    examples = height * groups
    dma = pltpu.SemaphoreType.DMA
    near_count, far_count = groups * rows_of_y, groups * max(rows_of_y - 1, 1)
    vmem = pl.BlockSpec(memory_space=pltpu.VMEM)
    return pl.pallas_call(
        functools.partial(share_kernel, rows_of_y, groups),
        out_shape=(
            jax.ShapeDtypeStruct((height, block), jnp.float32),
            jax.ShapeDtypeStruct((examples, examples), jnp.float32),
        ),
        in_specs=[vmem],
        out_specs=(vmem, vmem),
        scratch_shapes=[
            pltpu.VMEM((near_count, height, width), jnp.float32),
            pltpu.VMEM((far_count, height, width), jnp.float32),
            pltpu.VMEM((far_count, height, width), jnp.float32),
            pltpu.VMEM((examples, width), jnp.float32),
            dma((near_count,)),
            dma((near_count,)),
            dma((far_count,)),
            dma((far_count,)),
            dma((groups,)),
            dma((groups,)),
        ],
        compiler_params=pltpu.CompilerParams(
            collective_id=2, has_side_effects=True, vmem_limit_bytes=60 * 1024 * 1024
        ),
    )(partial_term)


def gram_kernel(sections, groups, count, tile_ref, out_ref, first, total, second, done, third, s1, r1, s2, r2, s3, r3):
    mine, place = lax.axis_index("param"), lax.axis_index("ex")
    height, width = out_ref.shape[0], total.shape[1]
    barrier = pltpu.get_barrier_semaphore()
    for d in range(1, sections):
        pl.semaphore_signal(
            barrier, inc=1, device_id={"param": lax.rem(mine + d, sections)}, device_id_type=pl.DeviceIdType.MESH
        )
    for d in range(1, groups):
        pl.semaphore_signal(
            barrier, inc=1, device_id={"ex": lax.rem(place + d, groups)}, device_id_type=pl.DeviceIdType.MESH
        )
    pl.semaphore_wait(barrier, sections + groups - 2)

    def send(axis, target, source, landing, send_sem, recv_sem, d):
        copy = pltpu.make_async_remote_copy(
            src_ref=source,
            dst_ref=landing.at[d - 1],
            send_sem=send_sem.at[d - 1],
            recv_sem=recv_sem.at[d - 1],
            device_id={axis: target},
            device_id_type=pl.DeviceIdType.MESH,
        )
        copy.start()
        return copy

    def columns(index):
        return pl.ds(pl.multiple_of(index * width, width), width)

    def lines(index):
        return pl.ds(pl.multiple_of(index * height, height), height)

    copies = []
    for d in range(1, sections):
        target = lax.rem(mine + d, sections)
        copies.append(send("param", target, tile_ref.at[:, columns(target)], first, s1, r1, d))
    total[...] = tile_ref[:, columns(mine)]
    for d, copy in enumerate(copies):
        copy.wait()
        total[...] += first[d]
    copies = []
    for d in range(1, groups):
        target = lax.rem(place + d, groups)
        copies.append(send("ex", target, total.at[lines(target), :], second, s2, r2, d))
    result = total[lines(place), :]
    for d, copy in enumerate(copies):
        copy.wait()
        result = result + second[d]
    done[...] = result / count
    copies = []
    for d in range(1, sections):
        copies.append(send("param", lax.rem(mine + d, sections), done, third, s3, r3, d))
    out_ref[:, columns(mine)] = done[...]
    for d, copy in enumerate(copies):
        copy.wait()
        out_ref[:, columns(lax.rem(mine + sections - d - 1, sections))] = third[d]


def reduce_gram(tile, count):
    sections, groups = lax.axis_size("param"), lax.axis_size("ex")
    examples = tile.shape[0]
    height, width = examples // groups, examples // sections
    dma = pltpu.SemaphoreType.DMA
    return pl.pallas_call(
        functools.partial(gram_kernel, sections, groups, count),
        out_shape=jax.ShapeDtypeStruct((height, examples), jnp.float32),
        in_specs=[pl.BlockSpec(memory_space=pltpu.VMEM)],
        out_specs=pl.BlockSpec(memory_space=pltpu.VMEM),
        scratch_shapes=[
            pltpu.VMEM((sections - 1, examples, width), jnp.float32),
            pltpu.VMEM((examples, width), jnp.float32),
            pltpu.VMEM((groups - 1, height, width), jnp.float32),
            pltpu.VMEM((height, width), jnp.float32),
            pltpu.VMEM((sections - 1, height, width), jnp.float32),
            dma((sections - 1,)),
            dma((sections - 1,)),
            dma((groups - 1,)),
            dma((groups - 1,)),
            dma((sections - 1,)),
            dma((sections - 1,)),
        ],
        compiler_params=pltpu.CompilerParams(collective_id=1, has_side_effects=True),
    )(tile)


def body(activations, cotangents, token_ids, signs, select):
    local_width = activations.shape[2]
    toks = activations.shape[1]
    slab_rows = cotangents.shape[2]
    section_count = lax.axis_size("param")
    width = local_width * section_count
    live_mask = token_ids != 0
    masked = jnp.where(live_mask[:, :, None], cotangents, jnp.zeros((), cotangents.dtype))
    lane_table = walsh_table(LANES).astype(jnp.bfloat16)
    mixed = mix_rows(masked, activations, signs)
    factor = 1.0 / float(toks * slab_rows * width) ** 0.5
    my_index = lax.axis_index("param")
    column = select % width
    row = select // width
    shared = column // local_width & my_index
    parity = jnp.zeros_like(shared)
    for bit_index in range(section_count.bit_length() - 1):
        parity = parity ^ shared >> bit_index & 1
    weight = (1 - 2 * parity).astype(jnp.float32) * factor
    half_rows = slab_rows // 2
    rows = row % half_rows * local_width + column % local_width
    upper = (row // half_rows).astype(jnp.float32)
    partial_term = pick_features(
        rows, mixed, jnp.concatenate([lane_table, lane_table], axis=1), upper[None, :], weight[None, :]
    )
    features, tile = share_features(partial_term)
    gram = reduce_gram(tile, select.shape[0])
    return (features, gram)


def solution(mesh):
    return jax.shard_map(
        body,
        mesh=mesh,
        in_specs=(
            P("ex", None, "param"),
            P("ex", None, None),
            P("ex", None),
            P(None, "param"),
            P(),
        ),
        out_specs=(P("ex", "param"), P("ex", None)),
        check_vma=False,
    )
```

```python
import functools

import jax
import jax.numpy as jnp
from jax import lax
from jax.experimental import pallas as pl
from jax.experimental.pallas import tpu as pltpu
from jax.sharding import PartitionSpec as P

LANES = 128
GROUP = 8


def walsh_table(table_order):
    row_index = lax.broadcasted_iota(jnp.int32, (table_order, table_order), 0)
    column_index = lax.broadcasted_iota(jnp.int32, (table_order, table_order), 1)
    common_bits = row_index & column_index
    parity = jnp.zeros((table_order, table_order), jnp.int32)
    for bit_index in range(table_order.bit_length() - 1):
        parity = parity ^ common_bits >> bit_index & 1
    return (1 - 2 * parity).astype(jnp.float32)


def split_two(value):
    high = value.astype(jnp.bfloat16)
    low = (value - high.astype(jnp.float32)).astype(jnp.bfloat16)
    return high, low


def butterfly(part):
    span = 1
    while span < len(part):
        part = [
            part[a] + part[a + span] if a & span == 0 else part[a - span] - part[a] for a in range(len(part))
        ]
        span *= 2
    return part


def mix_kernel(cots_ref, acts_ref, signs_ref, apart_ref, out_ref, held):
    slab_rows, group, block = out_ref.shape
    toks = cots_ref.shape[2]
    spread = jnp.concatenate([cots_ref[0]] * group, axis=1) * apart_ref[...]
    held[...] = jnp.dot(
        spread, acts_ref[...].reshape(group * toks, block), preferred_element_type=jnp.float32
    )
    radix = 8
    for c in range(block // LANES):
        lanes = slice(c * LANES, (c + 1) * LANES)
        flip = signs_ref[:, lanes].astype(jnp.float32)
        for high in range(slab_rows // radix):
            rows = [high * radix + j for j in range(radix)]
            part = butterfly([
                held[r * group:(r + 1) * group, lanes] * jnp.broadcast_to(flip[r:r + 1], (group, LANES))
                for r in rows
            ])
            for r, value in zip(rows, part):
                held[r * group:(r + 1) * group, lanes] = value
        for low in range(radix):
            rows = list(range(low, slab_rows, radix))
            part = butterfly([held[r * group:(r + 1) * group, lanes] for r in rows])
            for r, value in zip(rows, part):
                out_ref[r, :, lanes] = value


def mix_rows(cots, acts, signs):
    count_ex, toks, slab_rows = cots.shape
    width = acts.shape[2]
    block = min(width, 1024)
    spread = cots.reshape(count_ex // GROUP, GROUP, toks, slab_rows).transpose(0, 3, 1, 2)
    spread = spread.reshape(count_ex // GROUP, slab_rows * GROUP, toks)
    shape = (slab_rows * GROUP, GROUP * toks)
    apart = lax.broadcasted_iota(jnp.int32, shape, 0) % GROUP == lax.broadcasted_iota(jnp.int32, shape, 1) // toks
    return pl.pallas_call(
        mix_kernel,
        grid=(width // block, count_ex // GROUP),
        in_specs=[
            pl.BlockSpec((1, slab_rows * GROUP, toks), lambda c, e: (e, 0, 0)),
            pl.BlockSpec((GROUP, toks, block), lambda c, e: (e, 0, c)),
            pl.BlockSpec((slab_rows, block), lambda c, e: (0, c)),
            pl.BlockSpec(shape, lambda c, e: (0, 0)),
        ],
        out_specs=pl.BlockSpec((slab_rows, GROUP, block), lambda c, e: (0, e, c)),
        out_shape=jax.ShapeDtypeStruct((slab_rows, count_ex, width), jnp.float32),
        scratch_shapes=[pltpu.VMEM((slab_rows * GROUP, block), jnp.float32)],
    )(spread, acts, signs, apart.astype(jnp.bfloat16))


def pick_kernel(steps, rows_ref, mixed_ref, table_ref, upper_ref, weight_ref, out_ref, values, pieces, picked):
    step = pl.program_id(0)
    count_ex, width = mixed_ref.shape[2], mixed_ref.shape[3]
    blocks = width // LANES
    chunk = out_ref.shape[1]

    @pl.when(step < steps)
    def _():
        for half in range(2):
            for i in range(count_ex // 16):
                part = [
                    mixed_ref[half, 0, i * 16:(i + 1) * 16, a * LANES:(a + 1) * LANES] for a in range(blocks)
                ]
                span = 1
                while span < blocks:
                    part = [
                        part[a] + part[a + span] if a & span == 0 else part[a - span] - part[a]
                        for a in range(blocks)
                    ]
                    span *= 2
                row = half * count_ex + i * 16
                for a in range(blocks):
                    high, low = split_two(part[a])
                    pieces[row:row + 16, 2 * a * LANES:(2 * a + 1) * LANES] = high
                    pieces[row:row + 16, (2 * a + 1) * LANES:(2 * a + 2) * LANES] = low
        base = pl.multiple_of(step * width, LANES)
        for a in range(blocks):
            values[pl.ds(base + a * LANES, LANES), :] = lax.dot_general(
                table_ref[...],
                pieces[:, 2 * a * LANES:(2 * a + 2) * LANES],
                (((1,), (1,)), ((), ())),
                preferred_element_type=jnp.float32,
            )

    @pl.when(step >= steps)
    def _():
        start = (step - steps) * chunk

        def pick(i, carry):
            first = pl.multiple_of(i * 32, 32)
            taken = [values[pl.ds(rows_ref[start + first + j], 1), :] for j in range(32)]
            for j in range(32):
                picked[pl.ds(first + j, 1), :] = taken[j]
            return carry

        lax.fori_loop(0, chunk // 32, pick, 0)
        turned = picked[...].T
        out_ref[...] = jnp.where(upper_ref[...] > 0, turned[count_ex:], turned[:count_ex]) * weight_ref[...]


def pick_features(rows, mixed, table, upper, weight):
    slab_rows, count_ex, width = mixed.shape
    count = rows.shape[0]
    steps = slab_rows // 2
    chunk = min(count, 1024)
    halves = mixed.reshape(2, steps, count_ex, width)
    return pl.pallas_call(
        functools.partial(pick_kernel, steps),
        grid_spec=pltpu.PrefetchScalarGridSpec(
            num_scalar_prefetch=1,
            grid=(steps + count // chunk,),
            in_specs=[
                pl.BlockSpec((2, 1, count_ex, width), lambda s, rows: (0, jnp.minimum(s, steps - 1), 0, 0)),
                pl.BlockSpec(table.shape, lambda s, rows: (0, 0)),
                pl.BlockSpec((1, chunk), lambda s, rows: (0, jnp.maximum(s - steps, 0))),
                pl.BlockSpec((1, chunk), lambda s, rows: (0, jnp.maximum(s - steps, 0))),
            ],
            out_specs=pl.BlockSpec((count_ex, chunk), lambda s, rows: (0, jnp.maximum(s - steps, 0))),
            scratch_shapes=[
                pltpu.VMEM((steps * width, LANES), jnp.float32),
                pltpu.VMEM((2 * count_ex, 2 * width), jnp.bfloat16),
                pltpu.VMEM((chunk, LANES), jnp.float32),
            ],
        ),
        out_shape=jax.ShapeDtypeStruct((count_ex, count), jnp.float32),
        compiler_params=pltpu.CompilerParams(vmem_limit_bytes=60 * 1024 * 1024),
    )(rows, halves, table, upper, weight)


def share_kernel(
    rows_of_y, groups, part_ref, out_ref, tile_ref, near, sums, far, whole, near_s, near_r, far_s, far_r, ex_s, ex_r
):
    mine, place = lax.axis_index("param"), lax.axis_index("ex")
    my_y, my_core = mine // 2, lax.rem(mine, 2)
    height, block = out_ref.shape
    width = block // groups
    barrier = pltpu.get_barrier_semaphore()
    mesh_type = pl.DeviceIdType.MESH

    def owner(dy, core):
        return lax.rem(my_y + dy, rows_of_y) * 2 + core

    pl.semaphore_signal(barrier, inc=1, device_id={"param": owner(0, 1 - my_core)}, device_id_type=mesh_type)
    for dy in range(1, rows_of_y):
        pl.semaphore_signal(barrier, inc=1, device_id={"param": owner(dy, my_core)}, device_id_type=mesh_type)
    for d in range(1, groups):
        pl.semaphore_signal(
            barrier, inc=1, device_id={"ex": lax.rem(place + d, groups)}, device_id_type=mesh_type
        )
    pl.semaphore_wait(barrier, rows_of_y + groups - 1)

    def part(dy, core, slot):
        start = owner(dy, core) * block + slot * width
        return (slice(None), pl.ds(pl.multiple_of(start, width), width))

    def send(target, source, landing, send_sem, recv_sem):
        copy = pltpu.make_async_remote_copy(
            src_ref=source,
            dst_ref=landing,
            send_sem=send_sem,
            recv_sem=recv_sem,
            device_id=target,
            device_id_type=mesh_type,
        )
        copy.start()
        return copy

    order = list(range(1, groups)) + [0]
    slots = {m: lax.rem(place + m, groups) for m in order}
    offsets = list(range(1, rows_of_y)) + [0]
    near_copies, far_copies, ex_copies = {}, {}, {}
    for m in order:
        for dy in offsets:
            n = m * rows_of_y + dy
            near_copies[m, dy] = send(
                {"param": owner(0, 1 - my_core)},
                part_ref.at[part(dy, 1 - my_core, slots[m])],
                near.at[n],
                near_s.at[n],
                near_r.at[n],
            )
    for m in order:
        for dy in offsets:
            near_copies[m, dy].wait_recv()
            joined = part_ref[part(dy, my_core, slots[m])] + near[m * rows_of_y + dy]
            if dy == 0:
                out_ref[:, pl.ds(pl.multiple_of(slots[m] * width, width), width)] = joined
            else:
                n = m * (rows_of_y - 1) + dy - 1
                sums[n] = joined
                far_copies[m, dy] = send(
                    {"param": owner(dy, my_core)}, sums.at[n], far.at[n], far_s.at[n], far_r.at[n]
                )
    my_lines = pl.ds(pl.multiple_of(place * height, height), height)
    for m in order:
        here = pl.ds(pl.multiple_of(slots[m] * width, width), width)
        joined = out_ref[:, here]
        for dy in range(1, rows_of_y):
            far_copies[m, dy].wait_recv()
            joined = joined + far[m * (rows_of_y - 1) + dy - 1]
        out_ref[:, here] = joined
        if m == 0:
            whole[my_lines, :] = joined
        else:
            ex_copies[m] = send(
                {"ex": slots[m]}, out_ref.at[:, here], whole.at[my_lines, :], ex_s.at[m], ex_r.at[m]
            )
    for copy in near_copies.values():
        copy.wait_send()
    for copy in far_copies.values():
        copy.wait_send()
    for copy in ex_copies.values():
        copy.wait()
    high, low = split_two(whole[...])

    def inner(left, right):
        return lax.dot_general(left, right, (((1,), (1,)), ((), ())), preferred_element_type=jnp.float32)

    tile_ref[...] = inner(high, low) + inner(low, high) + inner(high, high)


def share_features(partial_term):
    sections, groups = lax.axis_size("param"), lax.axis_size("ex")
    height, count = partial_term.shape
    rows_of_y = sections // 2
    block = count // sections
    width = block // groups
    examples = height * groups
    dma = pltpu.SemaphoreType.DMA
    near_count, far_count = groups * rows_of_y, groups * max(rows_of_y - 1, 1)
    vmem = pl.BlockSpec(memory_space=pltpu.VMEM)
    return pl.pallas_call(
        functools.partial(share_kernel, rows_of_y, groups),
        out_shape=(
            jax.ShapeDtypeStruct((height, block), jnp.float32),
            jax.ShapeDtypeStruct((examples, examples), jnp.float32),
        ),
        in_specs=[vmem],
        out_specs=(vmem, vmem),
        scratch_shapes=[
            pltpu.VMEM((near_count, height, width), jnp.float32),
            pltpu.VMEM((far_count, height, width), jnp.float32),
            pltpu.VMEM((far_count, height, width), jnp.float32),
            pltpu.VMEM((examples, width), jnp.float32),
            dma((near_count,)),
            dma((near_count,)),
            dma((far_count,)),
            dma((far_count,)),
            dma((groups,)),
            dma((groups,)),
        ],
        compiler_params=pltpu.CompilerParams(
            collective_id=2, has_side_effects=True, vmem_limit_bytes=60 * 1024 * 1024
        ),
    )(partial_term)


def gram_kernel(
    sections, groups, count, tile_ref, out_ref, near, sums, first, total, second, done, third,
    s0, r0, s1, r1, s2, r2, s3, r3,
):
    mine, place = lax.axis_index("param"), lax.axis_index("ex")
    height, width = out_ref.shape[0], total.shape[1]
    barrier = pltpu.get_barrier_semaphore()
    for d in range(1, sections):
        pl.semaphore_signal(
            barrier, inc=1, device_id={"param": lax.rem(mine + d, sections)}, device_id_type=pl.DeviceIdType.MESH
        )
    for d in range(1, groups):
        pl.semaphore_signal(
            barrier, inc=1, device_id={"ex": lax.rem(place + d, groups)}, device_id_type=pl.DeviceIdType.MESH
        )
    pl.semaphore_wait(barrier, sections + groups - 2)

    def send(axis, target, source, landing, send_sem, recv_sem, d):
        copy = pltpu.make_async_remote_copy(
            src_ref=source,
            dst_ref=landing.at[d - 1],
            send_sem=send_sem.at[d - 1],
            recv_sem=recv_sem.at[d - 1],
            device_id={axis: target},
            device_id_type=pl.DeviceIdType.MESH,
        )
        copy.start()
        return copy

    def columns(index):
        return pl.ds(pl.multiple_of(index * width, width), width)

    def lines(index):
        return pl.ds(pl.multiple_of(index * height, height), height)

    rows_of_y = sections // 2
    my_core = lax.rem(mine, 2)

    def owner(dy, core):
        return lax.rem(mine // 2 + dy, rows_of_y) * 2 + core

    near_copies, copies = {}, []
    offsets = list(range(1, rows_of_y)) + [0]
    for dy in offsets:
        source = tile_ref.at[:, columns(owner(dy, 1 - my_core))]
        near_copies[dy] = send("param", owner(0, 1 - my_core), source, near, s0, r0, dy + 1)
    for dy in offsets:
        near_copies[dy].wait()
        joined = tile_ref[:, columns(owner(dy, my_core))] + near[dy]
        if dy == 0:
            total[...] = joined
        else:
            sums[dy - 1] = joined
            copies.append(send("param", owner(dy, my_core), sums.at[dy - 1], first, s1, r1, dy))
    for d, copy in enumerate(copies):
        copy.wait()
        total[...] += first[d]
    copies = []
    for d in range(1, groups):
        target = lax.rem(place + d, groups)
        copies.append(send("ex", target, total.at[lines(target), :], second, s2, r2, d))
    result = total[lines(place), :]
    for d, copy in enumerate(copies):
        copy.wait()
        result = result + second[d]
    done[...] = result / count
    copies = []
    for d in range(1, sections):
        copies.append(send("param", lax.rem(mine + d, sections), done, third, s3, r3, d))
    out_ref[:, columns(mine)] = done[...]
    for d, copy in enumerate(copies):
        copy.wait()
        out_ref[:, columns(lax.rem(mine + sections - d - 1, sections))] = third[d]


def reduce_gram(tile, count):
    sections, groups = lax.axis_size("param"), lax.axis_size("ex")
    examples = tile.shape[0]
    height, width = examples // groups, examples // sections
    dma = pltpu.SemaphoreType.DMA
    return pl.pallas_call(
        functools.partial(gram_kernel, sections, groups, count),
        out_shape=jax.ShapeDtypeStruct((height, examples), jnp.float32),
        in_specs=[pl.BlockSpec(memory_space=pltpu.VMEM)],
        out_specs=pl.BlockSpec(memory_space=pltpu.VMEM),
        scratch_shapes=[
            pltpu.VMEM((sections // 2, examples, width), jnp.float32),
            pltpu.VMEM((max(sections // 2 - 1, 1), examples, width), jnp.float32),
            pltpu.VMEM((max(sections // 2 - 1, 1), examples, width), jnp.float32),
            pltpu.VMEM((examples, width), jnp.float32),
            pltpu.VMEM((groups - 1, height, width), jnp.float32),
            pltpu.VMEM((height, width), jnp.float32),
            pltpu.VMEM((sections - 1, height, width), jnp.float32),
            dma((sections // 2,)),
            dma((sections // 2,)),
            dma((max(sections // 2 - 1, 1),)),
            dma((max(sections // 2 - 1, 1),)),
            dma((groups - 1,)),
            dma((groups - 1,)),
            dma((sections - 1,)),
            dma((sections - 1,)),
        ],
        compiler_params=pltpu.CompilerParams(collective_id=1, has_side_effects=True),
    )(tile)


def body(activations, cotangents, token_ids, signs, select):
    local_width = activations.shape[2]
    toks = activations.shape[1]
    slab_rows = cotangents.shape[2]
    section_count = lax.axis_size("param")
    width = local_width * section_count
    live_mask = token_ids != 0
    masked = jnp.where(live_mask[:, :, None], cotangents, jnp.zeros((), cotangents.dtype))
    lane_table = walsh_table(LANES).astype(jnp.bfloat16)
    mixed = mix_rows(masked, activations, signs)
    factor = 1.0 / float(toks * slab_rows * width) ** 0.5
    my_index = lax.axis_index("param")
    column = select % width
    row = select // width
    shared = column // local_width & my_index
    parity = jnp.zeros_like(shared)
    for bit_index in range(section_count.bit_length() - 1):
        parity = parity ^ shared >> bit_index & 1
    weight = (1 - 2 * parity).astype(jnp.float32) * factor
    half_rows = slab_rows // 2
    rows = row % half_rows * local_width + column % local_width
    upper = (row // half_rows).astype(jnp.float32)
    partial_term = pick_features(
        rows, mixed, jnp.concatenate([lane_table, lane_table], axis=1), upper[None, :], weight[None, :]
    )
    features, tile = share_features(partial_term)
    gram = reduce_gram(tile, select.shape[0])
    return (features, gram)


def solution(mesh):
    return jax.shard_map(
        body,
        mesh=mesh,
        in_specs=(
            P("ex", None, "param"),
            P("ex", None, None),
            P("ex", None),
            P(None, "param"),
            P(),
        ),
        out_specs=(P("ex", "param"), P("ex", None)),
        check_vma=False,
    )
```
